256 devices in a mesh: grid: 32 (over z, y), var: 8 (over x, core).
Axes of the slice: x: 4, y: 4, z: 8, core: 2. Of those that a mesh axis runs over, the one named last changes fastest.
Arguments:
- data: bfloat16 [8, 1024, 49152], P('var', None, 'grid'), may hold values from -6 to 6
- area: float32 [49152], P('grid'), may hold values from 0.1 to 1
- eofs: bfloat16 [8, 49152, 128], P('var', 'grid'), may hold values from -0.02734375 to 0.02734375
- var_scale: float32 [8], P('var'), may hold values from 0.5 to 2
- recon_map: bfloat16 [8, 1024, 49152], P('var', None, 'grid'), may hold values from -0.1875 to 0.1875
Outputs:
- fields: bfloat16 [8, 1024, 49152], P('var', None, 'grid')
The draws below stay inside these ranges and needn't reach their ends.
All inputs are finite; a program needn't handle non-finite values.
Results may differ from the reference program's by a relative error of at most 0.0057.
Values may be sent and summed in bfloat16 or wider, within the bound.
No kernel may reach another device: no remote copies, remote signals or barrier semaphores. Data moves between devices by JAX's collectives and lax.ppermute only.
A program may use at most 64 MiB of HBM per device.

```python
import math
import jax
import jax.numpy as jnp
from jax import lax

T_STEPS = 1024
K = 128
VARS = 8
JOINED = 1024
GRID = 49152


def strengthened(drawn, key, source, target, parts, factor):
    owner, partner = [(jnp.arange(drawn.shape[axis_at]) // (drawn.shape[axis_at] // parts)).reshape([-1 if axis == axis_at else 1 for axis in range(drawn.ndim)]) for axis_at in (source, target)]
    chosen = jax.random.permutation(key, parts)[partner]
    strong = (owner == chosen) | (owner == (partner + parts // 2) % parts)
    return jnp.where(strong, factor * drawn, drawn)


def steps_of(own_key, extent, pieces, least, high):
    factor_of, own = 1.0, jax.random.fold_in(own_key, 6)
    for dim, shards_of in pieces:
        heights = jnp.exp(jax.random.uniform(jax.random.fold_in(own, dim), (shards_of,), jnp.float32, least / len(pieces), high / len(pieces)))
        factor_of = factor_of * jnp.repeat(heights, extent[dim] // shards_of).reshape([-1 if axis == dim else 1 for axis in range(len(extent))])
    return factor_of


def scatter_about(own_key, extent, width, limit, shards=(), held_as=jnp.bfloat16):
    loudness = steps_of(own_key, extent, shards, -0.22, 0.18) if shards else 1.0
    values = jax.random.normal(own_key, extent, jnp.float32) * width * loudness
    return jnp.minimum(jnp.maximum(values, -limit), limit).astype(held_as)


def heavy_noise(key, dims, deviation, reach, cuts, heavy, kind=jnp.bfloat16):
    values = deviation * jax.random.normal(key, dims, jnp.float32)
    if cuts:
        values = values * steps_of(key, dims, cuts, -0.22, 0.18)
    return jnp.clip(strengthened(values, jax.random.fold_in(key, 3), *heavy), -reach, reach).astype(kind)


def setup_inputs(seed: int = 0) -> dict:
    keys = jax.random.split(jax.random.key(seed), 6)
    return {
        "data": heavy_noise(keys[0], (VARS, T_STEPS, GRID), 1.0, 6.0, ((0, 8), (2, 32)), (2, 1, 32, 2.75)),
        "area": jnp.clip(jnp.exp(math.log(1.0) - 2.3025851 * jax.random.uniform(keys[1], (GRID,), jnp.float32) ** steps_of(keys[1], (GRID,), ((0, 32),), -0.2, 0.2)), 0.1, 1.0),
        "eofs": scatter_about(keys[2], (VARS, GRID, K), GRID ** -0.5, 0.02734375, ((0, 8), (1, 32))),
        "var_scale": jnp.clip(jnp.exp(math.log(2.0) - 1.3862944 * jax.random.uniform(keys[3], (VARS,), jnp.float32) ** steps_of(keys[3], (VARS,), ((0, 8),), -0.2, 0.2)), 0.5, 2.0),
        "recon_map": scatter_about(keys[4], (VARS, JOINED, GRID), JOINED ** -0.5, 0.1875, ((0, 8), (2, 32))),
    }


def reference(data, area, eofs, var_scale, recon_map):
    scaled = (area[None, :, None] * eofs.astype(jnp.float32)).astype(jnp.bfloat16)

    def project(pair):
        return jnp.dot(pair[0], pair[1], preferred_element_type=jnp.float32)

    comps = lax.map(project, (data, scaled))
    weighted = (var_scale[:, None, None] * comps).astype(jnp.bfloat16)
    joined = jnp.transpose(weighted, (1, 0, 2)).reshape(T_STEPS, JOINED)

    def rebuild(pattern):
        return jnp.dot(joined, pattern, preferred_element_type=jnp.float32).astype(jnp.bfloat16)

    return lax.map(rebuild, recon_map)
```

```python
import jax
import jax.numpy as jnp
from jax import lax
from jax.sharding import Mesh, PartitionSpec as P

GRID = ("z", "y")


def gather(block, axes, count):
    spread = jnp.broadcast_to(block[None], (count, *block.shape))
    return lax.all_to_all(spread, axes, 0, 0, tiled=True)


def body(data, area, eofs, var_scale, recon_map):
    scaled = (area[:, None] * eofs[0].astype(jnp.float32)).astype(jnp.bfloat16)
    partial_comps = jnp.dot(data[0], scaled, preferred_element_type=jnp.float32)
    steps, modes = partial_comps.shape
    points = lax.axis_size("z") * lax.axis_size("y")
    pieces = partial_comps.astype(jnp.bfloat16).reshape(points, steps // points, modes)
    pieces = lax.all_to_all(pieces, GRID, 0, 0, tiled=True)
    comps = jnp.sum(pieces.astype(jnp.float32), axis=0)
    own = (var_scale[0] * comps).astype(jnp.bfloat16)
    mine = gather(own, GRID, points).reshape(steps, modes)
    across = gather(mine, "x", lax.axis_size("x"))
    other = lax.ppermute(across, "c", [(0, 1), (1, 0)])
    first = lax.axis_index("c") == 0
    both = jnp.stack([jnp.where(first, across, other), jnp.where(first, other, across)])
    joined = jnp.transpose(both, (2, 1, 0, 3)).reshape(steps, -1)
    rebuilt = jnp.dot(joined, recon_map[0], preferred_element_type=jnp.float32)
    return rebuilt.astype(jnp.bfloat16)[None]


def solution(mesh):
    fine = Mesh(mesh.devices.reshape(8, 4, 4, 2), ("z", "y", "x", "c"))
    var = ("x", "c")
    placed = (
        P(var, None, GRID),
        P(GRID),
        P(var, GRID, None),
        P(var),
        P(var, None, GRID),
    )
    return jax.shard_map(
        body, mesh=fine, in_specs=placed, out_specs=P(var, None, GRID), check_vma=False
    )
```

```python
import jax
import jax.numpy as jnp
from jax import lax
from jax.experimental import pallas as pl
from jax.experimental.pallas import tpu as pltpu
from jax.sharding import Mesh, PartitionSpec as P

GRID = ("z", "y")
ROWS = 256


def project_kernel(area_ref, eofs_ref, data_ref, out_ref, scaled):
    @pl.when(pl.program_id(0) == 0)
    def _():
        for i in range(area_ref.shape[0]):
            rows = pl.ds(i * 128, 128)
            weight = jnp.transpose(jnp.broadcast_to(area_ref[i : i + 1, :], (128, 128)))
            scaled[rows, :] = (weight * eofs_ref[rows, :].astype(jnp.float32)).astype(jnp.bfloat16)

    out_ref[...] = jnp.dot(
        data_ref[...], scaled[...], preferred_element_type=jnp.float32
    ).astype(jnp.bfloat16)


def project(area, eofs, data):
    steps, points = data.shape
    modes = eofs.shape[1]
    lanes = points // 128
    return pl.pallas_call(
        project_kernel,
        grid=(steps // ROWS,),
        in_specs=[
            pl.BlockSpec((lanes, 128), lambda i: (0, 0)),
            pl.BlockSpec((points, modes), lambda i: (0, 0)),
            pl.BlockSpec((ROWS, points), lambda i: (i, 0)),
        ],
        out_specs=pl.BlockSpec((ROWS, modes), lambda i: (i, 0)),
        out_shape=jax.ShapeDtypeStruct((steps, modes), jnp.bfloat16),
        scratch_shapes=[pltpu.VMEM((points, modes), jnp.bfloat16)],
        compiler_params=pltpu.CompilerParams(vmem_limit_bytes=32 << 20),
    )(area.reshape(lanes, 128), eofs, data)


def rebuild_kernel(*refs):
    blocks, (patterns_ref, out_ref) = refs[:-2], refs[-2:]
    x, c = lax.axis_index("x"), lax.axis_index("c")
    total = None
    for i in range(4):
        source = lax.rem(x + (0, 3, 1, 2)[i], 4) * 256
        own = pl.ds(pl.multiple_of(source + c * 128, 128), 128)
        other = pl.ds(pl.multiple_of(source + (1 - c) * 128, 128), 128)
        part = jnp.dot(
            jnp.concatenate([blocks[2 * i][...], blocks[2 * i + 1][...]], axis=1),
            jnp.concatenate([patterns_ref[own, :], patterns_ref[other, :]], axis=0),
            preferred_element_type=jnp.float32,
        )
        total = part if total is None else total + part
    out_ref[...] = total.astype(jnp.bfloat16)


def rebuild(blocks, patterns):
    steps, modes = blocks[0].shape
    joined, points = patterns.shape
    return pl.pallas_call(
        rebuild_kernel,
        grid=(steps // ROWS,),
        in_specs=[pl.BlockSpec((ROWS, modes), lambda i: (i, 0))] * len(blocks)
        + [pl.BlockSpec(memory_space=pltpu.VMEM)],
        out_specs=pl.BlockSpec((ROWS, points), lambda i: (i, 0)),
        out_shape=jax.ShapeDtypeStruct((steps, points), jnp.bfloat16),
        compiler_params=pltpu.CompilerParams(vmem_limit_bytes=48 << 20),
    )(*blocks, patterns)


def shift(block, axis, by):
    count = lax.axis_size(axis)
    return lax.ppermute(block, axis, [(i, (i + by) % count) for i in range(count)])


def body(data, area, eofs, var_scale, recon_map):
    partial_comps = project(area, eofs[0], data[0])
    steps, modes = partial_comps.shape
    points = lax.axis_size("z") * lax.axis_size("y")
    pieces = partial_comps.reshape(points, steps // points, modes)
    pieces = lax.all_to_all(pieces, GRID, 0, 0, tiled=True)
    comps = jnp.sum(pieces.astype(jnp.float32), axis=0)
    own = (var_scale[0] * comps).astype(jnp.bfloat16)
    spread = jnp.broadcast_to(own[None], (points, *own.shape))
    mine = lax.all_to_all(spread, GRID, 0, 0, tiled=True).reshape(steps, modes)
    blocks = [mine, shift(mine, "x", 1), shift(mine, "x", 3), shift(mine, "x", 2)]
    blocks = [part for block in blocks for part in (block, shift(block, "c", 1))]
    return rebuild(blocks, recon_map[0])[None]


def solution(mesh):
    fine = Mesh(mesh.devices.reshape(8, 4, 4, 2), ("z", "y", "x", "c"))
    var = ("x", "c")
    placed = (
        P(var, None, GRID),
        P(GRID),
        P(var, GRID, None),
        P(var),
        P(var, None, GRID),
    )
    return jax.shard_map(
        body, mesh=fine, in_specs=placed, out_specs=P(var, None, GRID), check_vma=False
    )
```

```python
import functools

import jax
import jax.numpy as jnp
from jax import lax
from jax.experimental import pallas as pl
from jax.experimental.pallas import tpu as pltpu
from jax.sharding import Mesh, PartitionSpec as P

GRID = ("z", "y")
ROWS = 256
COLUMNS = 512


def project_kernel(area_hbm, eofs_hbm, data_hbm, out_ref, area, eofs, scaled, data, sems):
    pieces = data_hbm.shape[0] // ROWS
    weights = pltpu.make_async_copy(area_hbm, area, sems.at[pieces + 1])
    weights.start()
    loads = [pltpu.make_async_copy(eofs_hbm, eofs, sems.at[pieces])]
    for i in range(pieces):
        rows = pl.ds(i * ROWS, ROWS)
        loads.append(pltpu.make_async_copy(data_hbm.at[rows, :], data.at[rows, :], sems.at[i]))
    for load in loads:
        load.start()
    weights.wait()
    loads[0].wait()
    for i in range(area.shape[0]):
        rows = pl.ds(i * 128, 128)
        weight = jnp.transpose(jnp.broadcast_to(area[i : i + 1, :], (128, 128)))
        scaled[rows, :] = (weight * eofs[rows, :].astype(jnp.float32)).astype(jnp.bfloat16)
    for i in range(pieces):
        rows = pl.ds(i * ROWS, ROWS)
        loads[1 + i].wait()
        out_ref[rows, :] = jnp.dot(
            data[rows, :], scaled[...], preferred_element_type=jnp.float32
        ).astype(jnp.bfloat16)


def project(area, eofs, data):
    steps, points = data.shape
    modes = eofs.shape[1]
    lanes = points // 128
    return pl.pallas_call(
        project_kernel,
        in_specs=[
            pl.BlockSpec(memory_space=pltpu.HBM),
            pl.BlockSpec(memory_space=pltpu.HBM),
            pl.BlockSpec(memory_space=pltpu.HBM),
        ],
        out_specs=pl.BlockSpec(memory_space=pltpu.VMEM),
        out_shape=pltpu.VMEM((steps, modes), jnp.bfloat16),
        scratch_shapes=[
            pltpu.VMEM((lanes, 128), jnp.float32),
            pltpu.VMEM((points, modes), jnp.bfloat16),
            pltpu.VMEM((points, modes), jnp.bfloat16),
            pltpu.VMEM((steps, points), jnp.bfloat16),
            pltpu.SemaphoreType.DMA((steps // ROWS + 2,)),
        ],
        compiler_params=pltpu.CompilerParams(vmem_limit_bytes=32 << 20),
    )(
        pltpu.with_memory_space_constraint(area.reshape(lanes, 128), pltpu.HBM),
        pltpu.with_memory_space_constraint(eofs, pltpu.HBM),
        pltpu.with_memory_space_constraint(data, pltpu.HBM),
    )


VMEM = pl.BlockSpec(memory_space=pltpu.VMEM)


def operands(blocks, sources, patterns_ref):
    x, c = lax.axis_index("x"), lax.axis_index("c")
    owners = []
    for source in sources:
        base = lax.rem(x + source, 4) * 256
        owners += [base + c * 128, base + (1 - c) * 128]
    owners = [pl.ds(pl.multiple_of(owner, 128), 128) for owner in owners]

    def joined(rows):
        return jnp.concatenate([block[rows, :] for block in blocks], axis=1)

    def patterns(columns):
        return jnp.concatenate([patterns_ref[k, columns] for k in owners], axis=0)

    return joined, patterns


def start_kernel(sources, *refs):
    blocks, patterns_ref, total_ref = refs[:-2], refs[-2], refs[-1]
    steps, points = total_ref.shape
    joined, patterns = operands(blocks, sources, patterns_ref)
    for i in range(steps // ROWS):
        rows = pl.ds(i * ROWS, ROWS)
        for j in range(points // COLUMNS):
            columns = pl.ds(j * COLUMNS, COLUMNS)
            total_ref[rows, columns] = jnp.dot(
                joined(rows), patterns(columns), preferred_element_type=jnp.float32
            )


def finish_kernel(sources, *refs):
    blocks, (patterns_ref, total_ref, out_hbm, out, sems) = refs[:-5], refs[-5:]
    steps, points = total_ref.shape
    joined, patterns = operands(blocks, sources, patterns_ref)
    stores = []
    for i in range(steps // 128):
        rows = pl.ds(i * 128, 128)
        for j in range(points // COLUMNS):
            columns = pl.ds(j * COLUMNS, COLUMNS)
            part = jnp.dot(joined(rows), patterns(columns), preferred_element_type=jnp.float32)
            out[rows, columns] = (total_ref[rows, columns] + part).astype(jnp.bfloat16)
        stores.append(pltpu.make_async_copy(out.at[rows, :], out_hbm.at[rows, :], sems.at[i]))
        stores[-1].start()
    for store in stores:
        store.wait()


def start(blocks, sources, patterns):
    steps, points = blocks[0].shape[0], patterns.shape[1]
    return pl.pallas_call(
        functools.partial(start_kernel, sources),
        in_specs=[VMEM] * (len(blocks) + 1),
        out_specs=VMEM,
        out_shape=pltpu.VMEM((steps, points), jnp.float32),
        compiler_params=pltpu.CompilerParams(vmem_limit_bytes=16 << 20),
    )(*blocks, patterns)


def finish(blocks, sources, patterns, total):
    steps, points = total.shape
    return pl.pallas_call(
        functools.partial(finish_kernel, sources),
        in_specs=[VMEM] * (len(blocks) + 2),
        out_specs=pl.BlockSpec(memory_space=pltpu.HBM),
        out_shape=jax.ShapeDtypeStruct((steps, points), jnp.bfloat16),
        scratch_shapes=[
            pltpu.VMEM((steps, points), jnp.bfloat16),
            pltpu.SemaphoreType.DMA((steps // 128,)),
        ],
        compiler_params=pltpu.CompilerParams(vmem_limit_bytes=16 << 20),
    )(*blocks, patterns, total)


def shift(block, axis, by):
    count = lax.axis_size(axis)
    return lax.ppermute(block, axis, [(i, (i + by) % count) for i in range(count)])


def exchange_and_rebuild(mine, patterns):
    blocks = [mine, shift(mine, "x", 2), shift(mine, "x", 1), shift(mine, "x", 3)]
    blocks = [(block, shift(block, "c", 1)) for block in blocks]
    early = [part for pair in blocks[:2] for part in pair]
    late = [part for pair in blocks[2:] for part in pair]
    total = start(early, (0, 2), patterns)
    return finish(late, (3, 1), patterns, total)


def body(data, area, eofs, var_scale, recon_map):
    partial_comps = project(area, eofs[0], data[0])
    patterns, partial_comps = lax.optimization_barrier((recon_map[0], partial_comps))
    steps, modes = partial_comps.shape
    points = lax.axis_size("z") * lax.axis_size("y")
    pieces = partial_comps.reshape(points, steps // points, modes)
    pieces = lax.all_to_all(pieces, GRID, 0, 0, tiled=True)
    comps = jnp.sum(pieces.astype(jnp.float32), axis=0)
    own = (var_scale[0] * comps).astype(jnp.bfloat16)
    spread = jnp.broadcast_to(own[None], (points, *own.shape))
    mine = lax.all_to_all(spread, GRID, 0, 0, tiled=True).reshape(steps, modes)
    return exchange_and_rebuild(mine, patterns)[None]


def solution(mesh):
    fine = Mesh(mesh.devices.reshape(8, 4, 4, 2), ("z", "y", "x", "c"))
    var = ("x", "c")
    placed = (
        P(var, None, GRID),
        P(GRID),
        P(var, GRID, None),
        P(var),
        P(var, None, GRID),
    )
    return jax.shard_map(
        body, mesh=fine, in_specs=placed, out_specs=P(var, None, GRID), check_vma=False
    )
```

```python
import functools

import jax
import jax.numpy as jnp
from jax import lax
from jax.experimental import pallas as pl
from jax.experimental.pallas import tpu as pltpu
from jax.sharding import Mesh, PartitionSpec as P

GRID = ("z", "y")
ROWS = 256
COLUMNS = 512


def project_kernel(weight_ref, area_hbm, eofs_hbm, data_hbm, out_ref, area, eofs, scaled, data, sems):
    pieces = data_hbm.shape[0] // ROWS
    weights = pltpu.make_async_copy(area_hbm, area, sems.at[pieces + 1])
    weights.start()
    loads = [pltpu.make_async_copy(eofs_hbm, eofs, sems.at[pieces])]
    for i in range(pieces):
        rows = pl.ds(i * ROWS, ROWS)
        loads.append(pltpu.make_async_copy(data_hbm.at[rows, :], data.at[rows, :], sems.at[i]))
    for load in loads:
        load.start()
    weights.wait()
    loads[0].wait()
    for i in range(area.shape[0]):
        rows = pl.ds(i * 128, 128)
        weight = jnp.transpose(jnp.broadcast_to(area[i : i + 1, :], (128, 128)))
        scaled[rows, :] = (weight * eofs[rows, :].astype(jnp.float32)).astype(jnp.bfloat16)
    for i in range(pieces):
        rows = pl.ds(i * ROWS, ROWS)
        loads[1 + i].wait()
        part = jnp.dot(data[rows, :], scaled[...], preferred_element_type=jnp.float32)
        out_ref[rows, :] = (weight_ref[0] * part).astype(jnp.bfloat16)


def project(weight, area, eofs, data):
    steps, points = data.shape
    modes = eofs.shape[1]
    lanes = points // 128
    return pl.pallas_call(
        project_kernel,
        in_specs=[
            pl.BlockSpec(memory_space=pltpu.SMEM),
            pl.BlockSpec(memory_space=pltpu.HBM),
            pl.BlockSpec(memory_space=pltpu.HBM),
            pl.BlockSpec(memory_space=pltpu.HBM),
        ],
        out_specs=pl.BlockSpec(memory_space=pltpu.VMEM),
        out_shape=pltpu.VMEM((steps, modes), jnp.bfloat16),
        scratch_shapes=[
            pltpu.VMEM((lanes, 128), jnp.float32),
            pltpu.VMEM((points, modes), jnp.bfloat16),
            pltpu.VMEM((points, modes), jnp.bfloat16),
            pltpu.VMEM((steps, points), jnp.bfloat16),
            pltpu.SemaphoreType.DMA((steps // ROWS + 2,)),
        ],
        compiler_params=pltpu.CompilerParams(vmem_limit_bytes=32 << 20),
    )(
        weight,
        pltpu.with_memory_space_constraint(area.reshape(lanes, 128), pltpu.HBM),
        pltpu.with_memory_space_constraint(eofs, pltpu.HBM),
        pltpu.with_memory_space_constraint(data, pltpu.HBM),
    )


VMEM = pl.BlockSpec(memory_space=pltpu.VMEM)


def operands(blocks, sources, patterns_ref):
    x, c = lax.axis_index("x"), lax.axis_index("c")
    owners = []
    for source in sources:
        base = lax.rem(x + source, 4) * 256
        owners += [base + c * 128, base + (1 - c) * 128]
    owners = [pl.ds(pl.multiple_of(owner, 128), 128) for owner in owners]

    def joined(rows):
        return jnp.concatenate([block[rows, :] for block in blocks], axis=1)

    def patterns(columns):
        return jnp.concatenate([patterns_ref[k, columns] for k in owners], axis=0)

    return joined, patterns


def start_kernel(sources, *refs):
    blocks, patterns_ref, total_ref = refs[:-2], refs[-2], refs[-1]
    steps, points = total_ref.shape
    joined, patterns = operands(blocks, sources, patterns_ref)
    for i in range(steps // ROWS):
        rows = pl.ds(i * ROWS, ROWS)
        for j in range(points // COLUMNS):
            columns = pl.ds(j * COLUMNS, COLUMNS)
            total_ref[rows, columns] = jnp.dot(
                joined(rows), patterns(columns), preferred_element_type=jnp.float32
            )


def finish_kernel(sources, *refs):
    blocks, (patterns_ref, total_ref, out_hbm, out, sems) = refs[:-5], refs[-5:]
    steps, points = total_ref.shape
    joined, patterns = operands(blocks, sources, patterns_ref)
    stores = []
    for i in range(steps // 128):
        rows = pl.ds(i * 128, 128)
        for j in range(points // COLUMNS):
            columns = pl.ds(j * COLUMNS, COLUMNS)
            part = jnp.dot(joined(rows), patterns(columns), preferred_element_type=jnp.float32)
            out[rows, columns] = (total_ref[rows, columns] + part).astype(jnp.bfloat16)
        stores.append(pltpu.make_async_copy(out.at[rows, :], out_hbm.at[rows, :], sems.at[i]))
        stores[-1].start()
    for store in stores:
        store.wait()


def start(blocks, sources, patterns):
    steps, points = blocks[0].shape[0], patterns.shape[1]
    return pl.pallas_call(
        functools.partial(start_kernel, sources),
        in_specs=[VMEM] * (len(blocks) + 1),
        out_specs=VMEM,
        out_shape=pltpu.VMEM((steps, points), jnp.float32),
        compiler_params=pltpu.CompilerParams(vmem_limit_bytes=16 << 20),
    )(*blocks, patterns)


def finish(blocks, sources, patterns, total):
    steps, points = total.shape
    return pl.pallas_call(
        functools.partial(finish_kernel, sources),
        in_specs=[VMEM] * (len(blocks) + 2),
        out_specs=pl.BlockSpec(memory_space=pltpu.HBM),
        out_shape=jax.ShapeDtypeStruct((steps, points), jnp.bfloat16),
        scratch_shapes=[
            pltpu.VMEM((steps, points), jnp.bfloat16),
            pltpu.SemaphoreType.DMA((steps // 128,)),
        ],
        compiler_params=pltpu.CompilerParams(vmem_limit_bytes=16 << 20),
    )(*blocks, patterns, total)


def shift(block, axis, by):
    count = lax.axis_size(axis)
    return lax.ppermute(block, axis, [(i, (i + by) % count) for i in range(count)])


def exchange_and_rebuild(mine, patterns):
    blocks = [mine, shift(mine, "x", 2), shift(mine, "x", 1), shift(mine, "x", 3)]
    blocks = [(block, shift(block, "c", 1)) for block in blocks]
    early = [part for pair in blocks[:2] for part in pair]
    late = [part for pair in blocks[2:] for part in pair]
    total = start(early, (0, 2), patterns)
    return finish(late, (3, 1), patterns, total)


def body(data, area, eofs, var_scale, recon_map):
    partial_comps = project(var_scale, area, eofs[0], data[0])
    patterns, partial_comps = lax.optimization_barrier((recon_map[0], partial_comps))
    steps, modes = partial_comps.shape
    points = lax.axis_size("z") * lax.axis_size("y")
    pieces = partial_comps.reshape(points, steps // points, modes)
    pieces = lax.all_to_all(pieces, GRID, 0, 0, tiled=True)
    comps = jnp.sum(pieces.astype(jnp.float32), axis=0)
    own = lax.reduce_precision(comps, 8, 7).astype(jnp.bfloat16)
    spread = jnp.broadcast_to(own[None], (points, *own.shape))
    mine = lax.all_to_all(spread, GRID, 0, 0, tiled=True).reshape(steps, modes)
    return exchange_and_rebuild(mine, patterns)[None]


def solution(mesh):
    fine = Mesh(mesh.devices.reshape(8, 4, 4, 2), ("z", "y", "x", "c"))
    var = ("x", "c")
    placed = (
        P(var, None, GRID),
        P(GRID),
        P(var, GRID, None),
        P(var),
        P(var, None, GRID),
    )
    return jax.shard_map(
        body, mesh=fine, in_specs=placed, out_specs=P(var, None, GRID), check_vma=False
    )
```

```python
import functools

import jax
import jax.numpy as jnp
from jax import lax
from jax.experimental import pallas as pl
from jax.experimental.pallas import tpu as pltpu
from jax.sharding import Mesh, PartitionSpec as P

GRID = ("z", "y")
ROWS = 256
COLUMNS = 512


def project_kernel(weight_ref, area_hbm, eofs_hbm, data_hbm, out_ref, area, eofs, scaled, data, sems):
    pieces = data_hbm.shape[0] // ROWS
    weights = pltpu.make_async_copy(area_hbm, area, sems.at[pieces + 1])
    weights.start()
    loads = [pltpu.make_async_copy(eofs_hbm, eofs, sems.at[pieces])]
    for i in range(pieces):
        rows = pl.ds(i * ROWS, ROWS)
        loads.append(pltpu.make_async_copy(data_hbm.at[rows, :], data.at[rows, :], sems.at[i]))
    for load in loads:
        load.start()
    weights.wait()
    loads[0].wait()
    for i in range(area.shape[0]):
        rows = pl.ds(i * 128, 128)
        weight = jnp.transpose(jnp.broadcast_to(area[i : i + 1, :], (128, 128)))
        scaled[rows, :] = (weight * eofs[rows, :].astype(jnp.float32)).astype(jnp.bfloat16)
    for i in range(pieces):
        rows = pl.ds(i * ROWS, ROWS)
        loads[1 + i].wait()
        part = jnp.dot(data[rows, :], scaled[...], preferred_element_type=jnp.float32)
        out_ref[rows, :] = (weight_ref[0] * part).astype(jnp.bfloat16)


def project(weight, area, eofs, data):
    steps, points = data.shape
    modes = eofs.shape[1]
    lanes = points // 128
    return pl.pallas_call(
        project_kernel,
        in_specs=[
            pl.BlockSpec(memory_space=pltpu.SMEM),
            pl.BlockSpec(memory_space=pltpu.HBM),
            pl.BlockSpec(memory_space=pltpu.HBM),
            pl.BlockSpec(memory_space=pltpu.HBM),
        ],
        out_specs=pl.BlockSpec(memory_space=pltpu.VMEM),
        out_shape=pltpu.VMEM((steps, modes), jnp.bfloat16),
        scratch_shapes=[
            pltpu.VMEM((lanes, 128), jnp.float32),
            pltpu.VMEM((points, modes), jnp.bfloat16),
            pltpu.VMEM((points, modes), jnp.bfloat16),
            pltpu.VMEM((steps, points), jnp.bfloat16),
            pltpu.SemaphoreType.DMA((steps // ROWS + 2,)),
        ],
        compiler_params=pltpu.CompilerParams(vmem_limit_bytes=32 << 20),
    )(
        weight,
        pltpu.with_memory_space_constraint(area.reshape(lanes, 128), pltpu.HBM),
        pltpu.with_memory_space_constraint(eofs, pltpu.HBM),
        pltpu.with_memory_space_constraint(data, pltpu.HBM),
    )


VMEM = pl.BlockSpec(memory_space=pltpu.VMEM)


def operands(blocks, sources, patterns_ref):
    x, c = lax.axis_index("x"), lax.axis_index("c")
    owners = []
    for source in sources:
        base = lax.rem(x + source, 4) * 256
        owners += [base + c * 128, base + (1 - c) * 128]
    owners = [pl.ds(pl.multiple_of(owner, 128), 128) for owner in owners]

    def joined(rows):
        return jnp.concatenate([block[rows, :] for block in blocks], axis=1)

    def patterns(columns):
        return jnp.concatenate([patterns_ref[k, columns] for k in owners], axis=0)

    return joined, patterns


def start_kernel(sources, *refs):
    blocks, patterns_ref, totals = refs[: 2 * len(sources)], refs[2 * len(sources)], refs[2 * len(sources) + 1 :]
    steps, points = totals[-1].shape
    joined, patterns = operands(blocks, sources, patterns_ref)
    for i in range(steps // ROWS):
        rows = pl.ds(i * ROWS, ROWS)
        for j in range(points // COLUMNS):
            columns = pl.ds(j * COLUMNS, COLUMNS)
            part = jnp.dot(joined(rows), patterns(columns), preferred_element_type=jnp.float32)
            totals[-1][rows, columns] = totals[0][rows, columns] + part if len(totals) > 1 else part


def finish_kernel(sources, *refs):
    blocks, (patterns_ref, total_ref, out_hbm, out, sems) = refs[:-5], refs[-5:]
    steps, points = total_ref.shape
    joined, patterns = operands(blocks, sources, patterns_ref)
    stores = []
    for i in range(steps // 128):
        rows = pl.ds(i * 128, 128)
        for j in range(points // COLUMNS):
            columns = pl.ds(j * COLUMNS, COLUMNS)
            part = jnp.dot(joined(rows), patterns(columns), preferred_element_type=jnp.float32)
            out[rows, columns] = (total_ref[rows, columns] + part).astype(jnp.bfloat16)
        stores.append(pltpu.make_async_copy(out.at[rows, :], out_hbm.at[rows, :], sems.at[i]))
        stores[-1].start()
    for store in stores:
        store.wait()


def start(blocks, sources, patterns, total=()):
    steps, points = blocks[0].shape[0], patterns.shape[1]
    return pl.pallas_call(
        functools.partial(start_kernel, sources),
        in_specs=[VMEM] * (len(blocks) + 1 + len(total)),
        out_specs=VMEM,
        out_shape=pltpu.VMEM((steps, points), jnp.float32),
        input_output_aliases={len(blocks) + 1: 0} if total else {},
        compiler_params=pltpu.CompilerParams(vmem_limit_bytes=16 << 20),
    )(*blocks, patterns, *total)


def finish(blocks, sources, patterns, total):
    steps, points = total.shape
    return pl.pallas_call(
        functools.partial(finish_kernel, sources),
        in_specs=[VMEM] * (len(blocks) + 2),
        out_specs=pl.BlockSpec(memory_space=pltpu.HBM),
        out_shape=jax.ShapeDtypeStruct((steps, points), jnp.bfloat16),
        scratch_shapes=[
            pltpu.VMEM((steps, points), jnp.bfloat16),
            pltpu.SemaphoreType.DMA((steps // 128,)),
        ],
        compiler_params=pltpu.CompilerParams(vmem_limit_bytes=16 << 20),
    )(*blocks, patterns, total)


def shift(block, axis, by):
    count = lax.axis_size(axis)
    return lax.ppermute(block, axis, [(i, (i + by) % count) for i in range(count)])


def exchange_and_rebuild(mine, patterns):
    far, left, right = shift(mine, "x", 2), shift(mine, "x", 1), shift(mine, "x", 3)
    total = start([mine, shift(mine, "c", 1)], (0,), patterns)
    total = start([far, shift(far, "c", 1)], (2,), patterns, (total,))
    late = [left, shift(left, "c", 1), right, shift(right, "c", 1)]
    return finish(late, (3, 1), patterns, total)


def body(data, area, eofs, var_scale, recon_map):
    partial_comps = project(var_scale, area, eofs[0], data[0])
    patterns, partial_comps = lax.optimization_barrier((recon_map[0], partial_comps))
    steps, modes = partial_comps.shape
    points = lax.axis_size("z") * lax.axis_size("y")
    pieces = partial_comps.reshape(points, steps // points, modes)
    pieces = lax.all_to_all(pieces, GRID, 0, 0, tiled=True)
    comps = jnp.sum(pieces.astype(jnp.float32), axis=0)
    own = lax.reduce_precision(comps, 8, 7).astype(jnp.bfloat16)
    spread = jnp.broadcast_to(own[None], (points, *own.shape))
    mine = lax.all_to_all(spread, GRID, 0, 0, tiled=True).reshape(steps, modes)
    return exchange_and_rebuild(mine, patterns)[None]


def solution(mesh):
    fine = Mesh(mesh.devices.reshape(8, 4, 4, 2), ("z", "y", "x", "c"))
    var = ("x", "c")
    placed = (
        P(var, None, GRID),
        P(GRID),
        P(var, GRID, None),
        P(var),
        P(var, None, GRID),
    )
    return jax.shard_map(
        body, mesh=fine, in_specs=placed, out_specs=P(var, None, GRID), check_vma=False
    )
```
